512 devices in a mesh: ctx: 64 (over y, z), ch: 8 (over x, core).
Axes of the slice: x: 4, y: 4, z: 16, core: 2. Of those that a mesh axis runs over, the one named last changes fastest.
Arguments:
- query_input: bfloat16 [8192, 1024], P('ctx', 'ch'), may hold values from -6 to 6
- key_input: bfloat16 [8192, 1024], P('ctx', 'ch'), may hold values from -6 to 6
- value_input: bfloat16 [8192, 1024], P('ctx', 'ch'), may hold values from -6 to 6
- implicit_filter: float32 [8192, 1024], P('ctx', 'ch'), may hold values from -1.1 to 1.1
- explicit_taps: float32 [128, 1024], P(None, 'ch'), may hold values from -0.5 to 0.5
- skip_gain: float32 [1024], P('ch'), may hold values from -3 to 3
- out_grad: bfloat16 [8192, 1024], P('ctx', 'ch'), may hold values from -6 to 6
Outputs:
- mixed_output: float32 [8192, 1024], P('ctx', 'ch')
- query_grad: float32 [8192, 1024], P('ctx', 'ch')
- key_grad: float32 [8192, 1024], P('ctx', 'ch')
- value_grad: float32 [8192, 1024], P('ctx', 'ch')
- filter_grad: float32 [8192, 1024], P('ctx', 'ch')
- taps_grad: float32 [128, 1024], P(None, 'ch')
- skip_grad: float32 [1024], P('ch')
The draws below stay inside these ranges and needn't reach their ends.
All inputs are finite; a program needn't handle non-finite values.
Results may differ from the reference program's by a relative error of at most 0.0005.
Values sent between devices are 32-bit elements; how exact they have to be, the bound alone decides.
A program may use at most 64 MiB of HBM per device.

```python
import math
import jax
import jax.numpy as jnp
from jax import lax

MIXER_CHANNELS = 1024
MTAPS = 128
SEQUENCE_TOKENS = 8192


def draw_implicit_filter(key, part):
    rate_key = jax.random.fold_in(key, 11)
    spike_random_key = jax.random.fold_in(key, 12)
    rough_key = jax.random.fold_in(key, 13)
    token_location = jnp.arange(SEQUENCE_TOKENS, dtype=jnp.float32)[:, None]
    rate_draw = jax.random.uniform(rate_key, (1, MIXER_CHANNELS), jnp.float32)
    decay_reach_scale = 30.0 * jnp.exp(rate_draw * math.log(1000.0 * SEQUENCE_TOKENS / 30.0))
    noisy_component = jnp.clip(jax.random.normal(rough_key, (SEQUENCE_TOKENS, MIXER_CHANNELS), jnp.float32), -4.0, 4.0)
    filter_spikes = jax.random.randint(spike_random_key, (3, MIXER_CHANNELS), 0, SEQUENCE_TOKENS).astype(jnp.float32)
    spike_multiplier = jnp.where(token_location >= filter_spikes[0][None, :], 0.6, 1.0)
    spike_multiplier = spike_multiplier * jnp.where(token_location >= filter_spikes[1][None, :], 0.6, 1.0)
    spike_multiplier = spike_multiplier * jnp.where(token_location >= filter_spikes[2][None, :], 0.6, 1.0)
    filter_magnitude = 1.0 / jnp.sqrt(jnp.minimum(0.5 * decay_reach_scale, float(SEQUENCE_TOKENS)))
    return noisy_component * filter_magnitude * jnp.exp(-token_location / decay_reach_scale) * spike_multiplier


def block_scale(rng, extent, pieces, smallest, high):
    level, own = 1.0, jax.random.fold_in(rng, 6)
    for axis_at, parts in pieces:
        heights = jnp.exp(jax.random.uniform(jax.random.fold_in(own, axis_at), (parts,), jnp.float32, smallest / len(pieces), high / len(pieces)))
        level = level * jnp.repeat(heights, extent[axis_at] // parts).reshape([-1 if axis == axis_at else 1 for axis in range(len(extent))])
    return level


def noise(stream_key, extent, deviation, bound, split=(), held_as=jnp.bfloat16):
    array = jax.random.normal(stream_key, extent, jnp.float32) * deviation
    if len(split) > 0:
        array = block_scale(stream_key, extent, split, -0.22, 0.18) * array
    return jnp.clip(array, min=-bound, max=bound).astype(held_as)


def setup_inputs(seed: int = 0) -> dict:
    seeds = jax.random.split(jax.random.key(seed), 8)
    return {
        "query_input": noise(seeds[0], (SEQUENCE_TOKENS, MIXER_CHANNELS), 1.0, 6.0, ((0, 64), (1, 8))),
        "key_input": noise(seeds[1], (SEQUENCE_TOKENS, MIXER_CHANNELS), 1.0, 6.0, ((0, 64), (1, 8))),
        "value_input": noise(seeds[2], (SEQUENCE_TOKENS, MIXER_CHANNELS), 1.0, 6.0, ((0, 64), (1, 8))),
        "implicit_filter": draw_implicit_filter(jax.random.fold_in(seeds[7], 71), 0),
        "explicit_taps": noise(seeds[4], (MTAPS, MIXER_CHANNELS), MTAPS ** -0.5, 0.5, ((1, 8),), jnp.float32),
        "skip_gain": noise(seeds[5], (MIXER_CHANNELS,), 1.0, 3.0, ((0, 8),), jnp.float32),
        "out_grad": noise(seeds[6], (SEQUENCE_TOKENS, MIXER_CHANNELS), 1.0, 6.0, ((0, 64), (1, 8))),
    }


def causal_mix(signal, kernel):
    padded_size = 2 * signal.shape[0]
    spectrum = jnp.fft.rfft(signal, n=padded_size, axis=0) * jnp.fft.rfft(kernel, n=padded_size, axis=0)
    return jnp.fft.irfft(spectrum, n=padded_size, axis=0)[:signal.shape[0]]

def lagged_sum(later, earlier):
    padded_size = 2 * later.shape[0]
    spectrum = jnp.fft.rfft(later, n=padded_size, axis=0) * jnp.conj(jnp.fft.rfft(earlier, n=padded_size, axis=0))
    return jnp.fft.irfft(spectrum, n=padded_size, axis=0)[:later.shape[0]]

def reference(query_input, key_input, value_input, implicit_filter, explicit_taps, skip_gain, out_grad):
    query_full = query_input.astype(jnp.float32)
    key_full = key_input.astype(jnp.float32)
    value_full = value_input.astype(jnp.float32)
    grad_full = out_grad.astype(jnp.float32)
    product = key_full * value_full
    mix_grad = grad_full * query_full
    seq_length = product.shape[0]
    chan_width = product.shape[1]
    zero_rows = jnp.zeros((MTAPS, chan_width), product.dtype)
    padded_back = jnp.concatenate([zero_rows, product], axis=0)
    padded_ahead = jnp.concatenate([mix_grad, zero_rows], axis=0)

    def tap_step(tap_lag, loop_state):
        explicit_part, explicit_grad, tap_rows = loop_state
        tap_lag = tap_lag.astype(jnp.int32)
        behind_rows = lax.dynamic_slice_in_dim(padded_back, (MTAPS - tap_lag).astype(jnp.int32), seq_length, 0)
        ahead_rows = lax.dynamic_slice_in_dim(padded_ahead, tap_lag, seq_length, 0)
        tap_weight = lax.dynamic_slice_in_dim(explicit_taps, tap_lag, 1, 0)
        tap_row = lax.optimization_barrier(jnp.sum(mix_grad * behind_rows, axis=0, keepdims=True))
        return (explicit_part + tap_weight * behind_rows, explicit_grad + tap_weight * ahead_rows, lax.dynamic_update_slice_in_dim(tap_rows, tap_row, tap_lag, 0))
    start_state = (jnp.zeros_like(product), jnp.zeros_like(product), jnp.zeros((MTAPS, chan_width), product.dtype))
    explicit_part, explicit_grad, tap_rows = lax.fori_loop(0, MTAPS, tap_step, start_state)
    implicit_part = causal_mix(product, implicit_filter)
    mixer = implicit_part + explicit_part + skip_gain[None, :] * product
    mixed_output = query_full * mixer
    query_grad = grad_full * mixer
    product_grad = lagged_sum(mix_grad, implicit_filter) + explicit_grad + skip_gain[None, :] * mix_grad
    key_grad = product_grad * value_full
    value_grad = product_grad * key_full
    grad_scale = 1.0 / jnp.sqrt(jnp.float32(SEQUENCE_TOKENS))
    filter_grad = lagged_sum(mix_grad, product) * grad_scale
    taps_grad = tap_rows * grad_scale
    skip_grad = lax.optimization_barrier(jnp.sum(mix_grad * product, axis=0)) * grad_scale
    return (mixed_output, query_grad, key_grad, value_grad, filter_grad, taps_grad, skip_grad)
```

```python
import math

import jax
import jax.numpy as jnp
import numpy as np
from jax import lax
from jax.sharding import PartitionSpec as P


def tables(blocks, rows):
    s = np.arange(blocks)
    t = np.arange(rows)
    k1 = s + 0.25
    outer = 2 * np.pi * np.outer(k1, s) / blocks
    first = np.concatenate([np.cos(outer), -np.sin(outer)], axis=0)
    turn = 2 * np.pi * np.outer(k1, t) / (blocks * rows)
    inner = 2 * np.pi * (np.outer(t, t) % rows) / rows
    c, sn = np.cos(inner), np.sin(inner)
    wide = np.block([[c, -sn], [sn, c]])
    return (
        first.astype(np.float32),
        np.cos(turn).astype(np.float32),
        np.sin(turn).astype(np.float32),
        wide.astype(np.float32),
    )


def body(query_input, key_input, value_input, implicit_filter, explicit_taps, skip_gain, out_grad):
    rows, chans = query_input.shape
    n = lax.axis_size("ctx")
    me = lax.axis_index("ctx")
    mine = chans // n
    scale = 1.0 / math.sqrt(n * rows)
    first, cos_turn, sin_turn, wide = tables(n, rows)
    hi = lax.Precision.HIGHEST
    q = query_input.astype(jnp.float32)
    k = key_input.astype(jnp.float32)
    v = value_input.astype(jnp.float32)
    og = out_grad.astype(jnp.float32)
    prod = k * v
    mix = og * q
    extra = explicit_taps.at[0].add(skip_gain)
    filt = implicit_filter + jnp.where(me == 0, extra, 0.0)
    fields = jnp.stack([prod, filt, mix])
    sent = jnp.transpose(fields, (2, 0, 1)).reshape(n, mine, 3, rows)
    got = lax.all_to_all(sent, "ctx", 0, 0, tiled=True)
    a = jnp.einsum("ks,scft->kcft", first, got, precision=hi)
    ar, ai = a[:n], a[n:]
    ct, st = cos_turn[:, None, None, :], sin_turn[:, None, None, :]
    b = jnp.concatenate([ar * ct + ai * st, ai * ct - ar * st], axis=-1)
    x = jnp.einsum("kcft,tu->kcfu", b, wide, precision=hi)
    xr, xi = x[..., :rows], x[..., rows:]
    pr, pi, hr, hm, gr, gi = xr[:, :, 0], xi[:, :, 0], xr[:, :, 1], xi[:, :, 1], xr[:, :, 2], xi[:, :, 2]
    yr = jnp.stack([hr * pr - hm * pi, hr * gr + hm * gi, pr * gr + pi * gi], axis=2)
    yi = jnp.stack([hr * pi + hm * pr, hr * gi - hm * gr, pr * gi - pi * gr], axis=2)
    y = jnp.concatenate([yr, -yi], axis=-1)
    z = jnp.einsum("kcft,tu->kcfu", y, wide, precision=hi)
    zr, zi = z[..., :rows], -z[..., rows:]
    d = jnp.concatenate([zr * ct - zi * st, zi * ct + zr * st], axis=0)
    out = jnp.einsum("ks,kcft->scft", first * (1.0 / (n * rows)), d, precision=hi)
    lead = jnp.broadcast_to(out[:1, :, 2:], (n, mine, 1, rows))
    back = lax.all_to_all(jnp.concatenate([out, lead], axis=2), "ctx", 0, 0, tiled=True)
    res = jnp.transpose(back.reshape(chans, 4, rows), (1, 2, 0))
    mixer, pgrad, fgrad, tgrad = res[0], res[1], res[2] * scale, res[3] * scale
    return q * mixer, og * mixer, pgrad * v, pgrad * k, fgrad, tgrad, tgrad[0]


def solution(mesh):
    wide = P("ctx", "ch")
    return jax.shard_map(
        body,
        mesh=mesh,
        in_specs=(wide, wide, wide, wide, P(None, "ch"), P("ch"), wide),
        out_specs=(wide, wide, wide, wide, wide, P(None, "ch"), P("ch")),
        check_vma=False,
    )
```

```python
import functools
import math

import jax
import jax.numpy as jnp
import numpy as np
from jax import lax
from jax.experimental import pallas as pl
from jax.experimental.pallas import tpu as pltpu
from jax.sharding import PartitionSpec as P

HIGHEST = lax.Precision.HIGHEST


def tables(blocks, rows):
    s = np.arange(blocks)
    t = np.arange(rows)
    k1 = s + 0.25
    outer = 2 * np.pi * np.outer(k1, s) / blocks
    first = np.concatenate([np.cos(outer), -np.sin(outer)], axis=0)
    last = first.T / (blocks * rows)
    turn = 2 * np.pi * np.outer(k1, t) / (blocks * rows)
    turn = np.concatenate([np.cos(turn), np.sin(turn)], axis=1)
    inner = 2 * np.pi * (np.outer(t, t) % rows) / rows
    c, sn = np.cos(inner), np.sin(inner)
    wide = np.block([[c, -sn], [sn, c]])
    return tuple(jnp.asarray(a.astype(np.float32)) for a in (first, last, turn, wide))


def dot(a, b):
    return lax.dot_general(
        a, b, (((1,), (0,)), ((), ())), precision=HIGHEST, preferred_element_type=jnp.float32
    )


def peer_at(step, me, ny, nz):
    i = step // ny
    dy = step % ny
    mag = nz // 2 - (i + 1) // 2
    odd = i % 2
    dz = odd * mag + (1 - odd) * (nz - mag)
    z = (me % nz + dz) % nz
    y = (me // nz + dy) % ny
    return y * nz + z


def mix_kernel(
    n, nz,
    q_in, k_in, v_in, f_in, taps_in, skip_in, og_in, first_in, last_in, turn_in, wide_in,
    out,
    q, k, v, f, taps, skip, og, first, last, turn, wide,
    sent, got, back,
    load_sems, table_sem, own_sem, send_sem, recv_sem, send2_sem, recv2_sem,
):
    ny = n // nz
    me = lax.axis_index("ctx")
    ch = lax.axis_index("ch")
    loads = [
        pltpu.make_async_copy(src, dst, load_sems.at[i])
        for i, (src, dst) in enumerate(
            ((q_in, q), (k_in, k), (v_in, v), (f_in, f), (taps_in, taps), (skip_in, skip), (og_in, og))
        )
    ]
    fetch = [
        pltpu.make_async_copy(src, dst, table_sem.at[i])
        for i, (src, dst) in enumerate(((first_in, first), (last_in, last), (turn_in, turn), (wide_in, wide)))
    ]
    for copy in loads + fetch:
        copy.start()

    barrier = pltpu.get_barrier_semaphore()

    def greet(step, carry):
        pl.semaphore_signal(
            barrier, inc=1, device_id=(peer_at(step, me, ny, nz), ch), device_id_type=pl.DeviceIdType.MESH
        )
        return carry

    steps = n - ny
    lax.fori_loop(0, steps, greet, 0)
    lax.fori_loop(steps + 1, n, greet, 0)

    for copy in loads:
        copy.wait()
    prod = k[...].astype(jnp.float32) * v[...].astype(jnp.float32)
    mix = og[...].astype(jnp.float32) * q[...].astype(jnp.float32)
    rows = prod.shape[0]
    at_zero = lax.broadcasted_iota(jnp.int32, prod.shape, 0) == 0
    extra = taps[...] + jnp.where(at_zero, skip[...], 0.0)
    filt = f[...] + jnp.where(me == 0, extra, 0.0)
    for j, field in enumerate((prod, filt, mix)):
        turned = field.T
        for c in range(2):
            sent[pl.ds(2 * j + c, n, stride=6), :] = turned[c * n : (c + 1) * n]

    pl.semaphore_wait(barrier, n - 1)

    own = pltpu.make_async_copy(sent.at[pl.ds(6 * me, 6)], got.at[pl.ds(6 * me, 6)], own_sem)
    own.start()

    def push(src, dst, size, ssem, rsem):
        def go(step, carry):
            peer = peer_at(step, me, ny, nz)
            pltpu.make_async_remote_copy(
                src_ref=src.at[pl.ds(size * peer, size)],
                dst_ref=dst.at[pl.ds(size * me, size)],
                send_sem=ssem,
                recv_sem=rsem,
                device_id=(peer, ch),
                device_id_type=pl.DeviceIdType.MESH,
            ).start()
            return carry

        lax.fori_loop(0, steps, go, 0)
        lax.fori_loop(steps + 1, n, go, 0)

    def all_of(src, dst, size, ssem, rsem):
        return pltpu.make_async_remote_copy(
            src_ref=src.at[pl.ds(0, size * (n - 1))],
            dst_ref=dst.at[pl.ds(0, size * (n - 1))],
            send_sem=ssem,
            recv_sem=rsem,
            device_id=((me + 1) % n, ch),
            device_id_type=pl.DeviceIdType.MESH,
        )

    push(sent, got, 6, send_sem, recv_sem)
    for copy in fetch:
        copy.wait()
    own.wait()
    all_of(sent, got, 6, send_sem, recv_sem).wait_recv()

    x = jnp.concatenate([got[pl.ds(j, n, stride=6), :] for j in range(6)], axis=1)
    a = dot(first[...], x)
    ct, st = turn[:, :rows], turn[:, rows:]
    parts = []
    for j in range(6):
        ar = a[:n, j * rows : (j + 1) * rows]
        ai = a[n:, j * rows : (j + 1) * rows]
        parts.append(jnp.concatenate([ar * ct + ai * st, ai * ct - ar * st], axis=1))
    w = wide[...]
    x = dot(jnp.concatenate(parts, axis=0), w)

    def spectrum(j):
        block = x[j * n : (j + 1) * n]
        return block[:, :rows], block[:, rows:]

    parts = [None] * 6
    for c in range(2):
        (pr, pi), (hr, hi), (gr, gi) = spectrum(c), spectrum(2 + c), spectrum(4 + c)
        parts[c] = jnp.concatenate([pr * gr + pi * gi, pi * gr - pr * gi], axis=1)
        parts[2 + c] = jnp.concatenate([hr * pr - hi * pi, -hr * pi - hi * pr], axis=1)
        parts[4 + c] = jnp.concatenate([hr * gr + hi * gi, hi * gr - hr * gi], axis=1)
    z = dot(jnp.concatenate(parts, axis=0), w)
    res, ims = [], []
    for j in range(6):
        zr = z[j * n : (j + 1) * n, :rows]
        zi = z[j * n : (j + 1) * n, rows:]
        res.append(zr * ct + zi * st)
        ims.append(zr * st - zi * ct)
    d = jnp.concatenate([jnp.concatenate(res, axis=1), jnp.concatenate(ims, axis=1)], axis=0)
    y = dot(last[...], d)
    for j in range(6):
        piece = y[:, j * rows : (j + 1) * rows]
        back[pl.ds(j, n, stride=8), :] = piece
        if j < 2:
            back[pl.ds(6 + j, n, stride=8), :] = jnp.broadcast_to(piece[:1], (n, rows))

    own = pltpu.make_async_copy(back.at[pl.ds(8 * me, 8)], out.at[pl.ds(8 * me, 8)], own_sem)
    own.start()
    push(back, out, 8, send2_sem, recv2_sem)
    own.wait()
    all_of(back, out, 8, send2_sem, recv2_sem).wait_recv()
    all_of(sent, got, 6, send_sem, recv_sem).wait_send()
    all_of(back, out, 8, send2_sem, recv2_sem).wait_send()


def close_kernel(n, scale, got, q, k, v, og, *refs):
    outs, bufs, sems = refs[:7], refs[7:14], refs[14]

    def whole(j):
        return jnp.concatenate([got[pl.ds(2 * j + c, n, stride=8), :] for c in range(2)], axis=0).T

    copies = [pltpu.make_async_copy(b, o, sems.at[i]) for i, (b, o) in enumerate(zip(bufs, outs))]
    lead = whole(3) * scale
    bufs[4][...] = whole(0) * scale
    bufs[5][...] = lead
    bufs[6][...] = lead[:1]
    mixer = whole(1)
    bufs[0][...] = q[...].astype(jnp.float32) * mixer
    bufs[1][...] = og[...].astype(jnp.float32) * mixer
    for i in (4, 5, 6, 0, 1):
        copies[i].start()
    pgrad = whole(2)
    bufs[2][...] = pgrad * v[...].astype(jnp.float32)
    bufs[3][...] = pgrad * k[...].astype(jnp.float32)
    for i in (2, 3):
        copies[i].start()
    for copy in copies:
        copy.wait()


def body(nz, query_input, key_input, value_input, implicit_filter, explicit_taps, skip_gain, out_grad):
    rows, chans = query_input.shape
    n = lax.axis_size("ctx")
    scale = 1.0 / math.sqrt(n * rows)
    first, last, turn, wide = tables(n, rows)
    f32, bf16 = jnp.float32, jnp.bfloat16
    vmem = pl.BlockSpec(memory_space=pltpu.VMEM)
    anywhere = pl.BlockSpec(memory_space=pl.ANY)
    tile = pltpu.VMEM((rows, chans), bf16)
    full = pltpu.VMEM((rows, chans), f32)
    got = pl.pallas_call(
        functools.partial(mix_kernel, n, nz),
        name="mix",
        out_shape=jax.ShapeDtypeStruct((8 * n, rows), f32),
        in_specs=[anywhere] * 11,
        out_specs=vmem,
        scratch_shapes=[
            tile, tile, tile, full, full, pltpu.VMEM((1, chans), f32), tile,
            *[pltpu.VMEM(t.shape, f32) for t in (first, last, turn, wide)],
            pltpu.VMEM((6 * n, rows), f32),
            pltpu.VMEM((6 * n, rows), f32),
            pltpu.VMEM((8 * n, rows), f32),
            pltpu.SemaphoreType.DMA((7,)),
            pltpu.SemaphoreType.DMA((4,)),
            *[pltpu.SemaphoreType.DMA] * 5,
        ],
        compiler_params=pltpu.CompilerParams(collective_id=0, has_side_effects=True),
    )(
        query_input, key_input, value_input, implicit_filter, explicit_taps,
        skip_gain.reshape(1, chans), out_grad, first, last, turn, wide,
    )
    wide_out = jax.ShapeDtypeStruct((rows, chans), f32)
    outs = pl.pallas_call(
        functools.partial(close_kernel, n, scale),
        name="close",
        out_shape=[wide_out] * 6 + [jax.ShapeDtypeStruct((1, chans), f32)],
        in_specs=[vmem] * 5,
        out_specs=[anywhere] * 7,
        scratch_shapes=[full] * 6 + [pltpu.VMEM((1, chans), f32), pltpu.SemaphoreType.DMA((7,))],
    )(got, query_input, key_input, value_input, out_grad)
    return (*outs[:6], outs[6].reshape(chans))


def solution(mesh):
    wide = P("ctx", "ch")
    nz = math.gcd(16, mesh.shape["ctx"])
    return jax.shard_map(
        functools.partial(body, nz),
        mesh=mesh,
        in_specs=(wide, wide, wide, wide, P(None, "ch"), P("ch"), wide),
        out_specs=(wide, wide, wide, wide, wide, P(None, "ch"), P("ch")),
        check_vma=False,
    )
```

```python
import functools
import math

import jax
import jax.numpy as jnp
import numpy as np
from jax import lax
from jax.experimental import pallas as pl
from jax.experimental.pallas import tpu as pltpu
from jax.sharding import PartitionSpec as P

F32, BF16 = jnp.float32, jnp.bfloat16
MESH = pl.DeviceIdType.MESH


def halves(table):
    high = table.astype(np.float32).astype(BF16)
    low = (table - high.astype(np.float64)).astype(np.float32).astype(BF16)
    return high, low


def tables(blocks, rows):
    s = np.arange(blocks)
    t = np.arange(rows)
    k1 = s + 0.25
    outer = 2 * np.pi * np.outer(k1, s) / blocks
    first = np.concatenate([np.cos(outer), -np.sin(outer)], axis=0)
    last = first.T / (blocks * rows)
    turn = 2 * np.pi * np.outer(k1, t) / (blocks * rows)
    turn = np.concatenate([np.cos(turn), np.sin(turn)], axis=1).astype(np.float32)
    inner = 2 * np.pi * (np.outer(t, t) % rows) / rows
    c, sn = np.cos(inner), np.sin(inner)
    wide = np.block([[c, -sn], [sn, c]])
    fh, fl = halves(first)
    lh, ll = halves(last)
    first3 = np.concatenate([fh, fh, fl], axis=1)
    last3 = np.concatenate([lh, lh, ll], axis=1)
    return tuple(jnp.asarray(a) for a in (first3, last3, turn, *halves(wide)))


def mm(a, b):
    return lax.dot_general(a, b, (((1,), (0,)), ((), ())), preferred_element_type=F32)


def split(x):
    high = x.astype(BF16)
    return high, (x - high.astype(F32)).astype(BF16)


def left(table3, x):
    high, low = split(x)
    return mm(table3, jnp.concatenate([high, low, high], axis=0))


def right(x, w_high, w_low):
    high, low = split(x)
    both = mm(jnp.concatenate([high, low], axis=0), w_high)
    return both[: x.shape[0]] + both[x.shape[0] :] + mm(high, w_low)


def far_first(i, nz):
    mag = nz // 2 - (i + 1) // 2
    odd = i % 2
    return odd * mag + (1 - odd) * (nz - mag)


def mix_kernel(
    n, nz,
    q_in, k_in, v_in, f_in, taps_in, skip_in, og_in, first_in, last_in, turn_in, wide_in, wlow_in,
    lag, main, lead, q, k, v, og,
    f, taps, skip, first, last, turn, wide, wlow,
    sent, got, lag_out, main_out, row,
    load_sems, table_sems, own_sems, send_sems, recv_sems,
):
    ny = n // nz
    me = lax.axis_index("ctx")
    ch = lax.axis_index("ch")
    my_z = me % nz
    my_y = me // nz
    loads = [
        pltpu.make_async_copy(src, dst, load_sems.at[i])
        for i, (src, dst) in enumerate(
            ((q_in, q), (k_in, k), (v_in, v), (f_in, f), (taps_in, taps), (skip_in, skip), (og_in, og))
        )
    ]
    fetch = [
        pltpu.make_async_copy(src, dst, table_sems.at[i])
        for i, (src, dst) in enumerate(
            ((first_in, first), (last_in, last), (turn_in, turn), (wide_in, wide), (wlow_in, wlow))
        )
    ]
    for copy in loads + fetch:
        copy.start()

    def peer_at(step):
        z = (my_z + far_first(step // ny, nz)) % nz
        y = (my_y + step % ny) % ny
        return y * nz + z

    def each_peer(visit):
        def go(step, carry):
            visit(peer_at(step))
            return carry

        away = n - ny
        lax.fori_loop(0, away, go, 0)
        lax.fori_loop(away + 1, n, go, 0)

    barrier = pltpu.get_barrier_semaphore()
    each_peer(lambda peer: pl.semaphore_signal(barrier, inc=1, device_id=(peer, ch), device_id_type=MESH))

    for copy in loads:
        copy.wait()
    prod = k[...].astype(F32) * v[...].astype(F32)
    mix = og[...].astype(F32) * q[...].astype(F32)
    rows = prod.shape[0]
    at_zero = lax.broadcasted_iota(jnp.int32, prod.shape, 0) == 0
    extra = taps[...] + jnp.where(at_zero, skip[...], 0.0)
    filt = f[...] + jnp.where(me == 0, extra, 0.0)
    for j, field in enumerate((prod, filt, mix)):
        turned = field.T
        for c in range(2):
            sent[pl.ds(2 * j + c, n, stride=6), :] = turned[c * n : (c + 1) * n]

    pl.semaphore_wait(barrier, n - 1)

    def remote(src, dst, i, peer):
        return pltpu.make_async_remote_copy(
            src_ref=src,
            dst_ref=dst,
            send_sem=send_sems.at[i],
            recv_sem=recv_sems.at[i],
            device_id=(peer, ch),
            device_id_type=MESH,
        )

    def push(src, dst, size, i):
        own = pltpu.make_async_copy(
            src.at[pl.ds(size * me, size)], dst.at[pl.ds(size * me, size)], own_sems.at[i]
        )
        own.start()
        each_peer(
            lambda peer: remote(
                src.at[pl.ds(size * peer, size)], dst.at[pl.ds(size * me, size)], i, peer
            ).start()
        )
        return own

    def total(src, dst, amount, i):
        return remote(src.at[pl.ds(0, amount)], dst.at[pl.ds(0, amount)], i, (me + 1) % n)

    own = push(sent, got, 6, 0)
    for copy in fetch:
        copy.wait()
    own.wait()
    forward = total(sent, got, 6 * (n - 1), 0)
    forward.wait_recv()

    x = jnp.concatenate([got[pl.ds(j, n, stride=6), :] for j in range(6)], axis=1)
    a = left(first[...], x)
    ct, st = turn[:, :rows], turn[:, rows:]
    parts = []
    for j in range(6):
        ar = a[:n, j * rows : (j + 1) * rows]
        ai = a[n:, j * rows : (j + 1) * rows]
        parts.append(jnp.concatenate([ar * ct + ai * st, ai * ct - ar * st], axis=1))
    x = right(jnp.concatenate(parts, axis=0), wide[...], wlow[...])

    def spectrum(j):
        block = x[j * n : (j + 1) * n]
        return block[:, :rows], block[:, rows:]

    def to_time(conjugates):
        z = right(jnp.concatenate(conjugates, axis=0), wide[...], wlow[...])
        res, ims = [], []
        for j in range(len(conjugates)):
            zr = z[j * n : (j + 1) * n, :rows]
            zi = z[j * n : (j + 1) * n, rows:]
            res.append(zr * ct + zi * st)
            ims.append(zr * st - zi * ct)
        d = jnp.concatenate([jnp.concatenate(res, axis=1), jnp.concatenate(ims, axis=1)], axis=0)
        y = left(last[...], d)
        return [y[:, j * rows : (j + 1) * rows] for j in range(len(conjugates))]

    def conj_of(ar, ai, br, bi):
        return jnp.concatenate([ar * br + ai * bi, ai * br - ar * bi], axis=1)

    spectra = [(spectrum(c), spectrum(2 + c), spectrum(4 + c)) for c in range(2)]
    for c, piece in enumerate(to_time([conj_of(*p, *g) for p, _, g in spectra])):
        lag_out[pl.ds(c, n, stride=2), :] = piece
        row[pl.ds(c, 1), :] = piece[:1]

    mine = pl.ds(pl.multiple_of(2 * my_z, 2), 2)
    near = lead.at[pl.ds(pl.multiple_of(2 * nz * my_y, 2 * nz), 2 * nz)]
    lead_own = pltpu.make_async_copy(row, near.at[mine], own_sems.at[3])
    lead_own.start()

    def along_z(i, carry):
        peer = my_y * nz + (my_z + far_first(i, nz)) % nz
        remote(row, near.at[mine], 3, peer).start()
        return carry

    lax.fori_loop(0, nz - 1, along_z, 0)
    lag_own = push(lag_out, lag, 2, 1)

    out = [jnp.concatenate([hr * pr - hi * pi, -(hr * pi + hi * pr)], axis=1) for (pr, pi), (hr, hi), _ in spectra]
    back = [conj_of(*h, *g) for _, h, g in spectra]
    for j, piece in enumerate(to_time(out + back)):
        main_out[pl.ds(j, n, stride=4), :] = piece
    main_own = push(main_out, main, 4, 2)

    lead_own.wait()
    by_z = remote(near.at[pl.ds(0, 2 * (nz - 1))], near.at[pl.ds(0, 2 * (nz - 1))], 3, (me + 1) % n)
    by_z.wait_recv()

    def along_y(step, carry):
        peer = (my_y + step) % ny * nz + my_z
        remote(near, near, 4, peer).start()
        return carry

    lax.fori_loop(1, ny, along_y, 0)

    lag_own.wait()
    main_own.wait()
    by_y = total(lead, lead, 2 * nz * (ny - 1), 4)
    lags = total(lag_out, lag, 2 * (n - 1), 1)
    mains = total(main_out, main, 4 * (n - 1), 2)
    lags.wait_recv()
    mains.wait_recv()
    by_y.wait_recv()
    for copy in (forward, lags, mains, by_z, by_y):
        copy.wait_send()


def close_kernel(n, scale, lag, main, lead, q, k, v, og, *refs):
    outs, bufs, sems = refs[:7], refs[7:14], refs[14]

    def whole(ref, j, step):
        return jnp.concatenate([ref[pl.ds(j + c, n, stride=step), :] for c in range(2)], axis=0).T

    copies = [pltpu.make_async_copy(b, o, sems.at[i]) for i, (b, o) in enumerate(zip(bufs, outs))]

    def put(i, value):
        bufs[i][...] = value
        copies[i].start()

    put(4, whole(lag, 0, 2) * scale)
    first_lags = whole(lead, 0, 2) * scale
    put(5, first_lags)
    put(6, first_lags[:1])
    mixer = whole(main, 0, 4)
    put(0, q[...].astype(F32) * mixer)
    put(1, og[...].astype(F32) * mixer)
    pgrad = whole(main, 2, 4)
    put(2, pgrad * v[...].astype(F32))
    put(3, pgrad * k[...].astype(F32))
    for copy in copies:
        copy.wait()


def body(nz, query_input, key_input, value_input, implicit_filter, explicit_taps, skip_gain, out_grad):
    rows, chans = query_input.shape
    n = lax.axis_size("ctx")
    scale = 1.0 / math.sqrt(n * rows)
    consts = tables(n, rows)
    vmem = pl.BlockSpec(memory_space=pltpu.VMEM)
    anywhere = pl.BlockSpec(memory_space=pl.ANY)
    tile = pltpu.VMEM((rows, chans), BF16)
    full = pltpu.VMEM((rows, chans), F32)
    one = pltpu.VMEM((1, chans), F32)

    def stack(count):
        return pltpu.VMEM((count, rows), F32)

    held = pl.pallas_call(
        functools.partial(mix_kernel, n, nz),
        name="mix",
        out_shape=[stack(2 * n), stack(4 * n), stack(2 * n), tile, tile, tile, tile],
        in_specs=[anywhere] * 12,
        out_specs=[vmem] * 7,
        scratch_shapes=[
            full, full, one,
            *[pltpu.VMEM(t.shape, t.dtype) for t in consts],
            stack(6 * n), stack(6 * n), stack(2 * n), stack(4 * n), stack(2),
            pltpu.SemaphoreType.DMA((7,)),
            pltpu.SemaphoreType.DMA((len(consts),)),
            pltpu.SemaphoreType.DMA((4,)),
            pltpu.SemaphoreType.DMA((5,)),
            pltpu.SemaphoreType.DMA((5,)),
        ],
        compiler_params=pltpu.CompilerParams(collective_id=0, has_side_effects=True),
    )(
        query_input, key_input, value_input, implicit_filter, explicit_taps,
        skip_gain.reshape(1, chans), out_grad, *consts,
    )
    held = [pltpu.with_memory_space_constraint(x, pltpu.VMEM) for x in held]
    wide_out = jax.ShapeDtypeStruct((rows, chans), F32)
    outs = pl.pallas_call(
        functools.partial(close_kernel, n, scale),
        name="close",
        out_shape=[wide_out] * 6 + [jax.ShapeDtypeStruct((1, chans), F32)],
        in_specs=[vmem] * 7,
        out_specs=[anywhere] * 7,
        scratch_shapes=[full] * 6 + [one, pltpu.SemaphoreType.DMA((7,))],
    )(*held)
    return (*outs[:6], outs[6].reshape(chans))


def solution(mesh):
    wide = P("ctx", "ch")
    nz = math.gcd(16, mesh.shape["ctx"])
    return jax.shard_map(
        functools.partial(body, nz),
        mesh=mesh,
        in_specs=(wide, wide, wide, wide, P(None, "ch"), P("ch"), wide),
        out_specs=(wide, wide, wide, wide, wide, P(None, "ch"), P("ch")),
        check_vma=False,
    )
```
